32 devices in a mesh: gx: 8 (over y, x, core), gy: 4 (over z).
Axes of the slice: x: 2, y: 2, z: 4, core: 2. Of those that a mesh axis runs over, the one named last changes fastest.
Arguments:
- coefficient: float32 [2, 2, 2, 64, 64, 128], P(None, None, None, 'gx', 'gy'), may hold values from 0.05 to 5
- owner: int32 [64, 64], P('gx', 'gy'), may hold values from 0 to 31, as said below
- w_in: bfloat16 [128, 27], replicated, may hold values from -1.25 to 1.25
- b_in: float32 [128], replicated, may hold values from -3 to 3
- w_mid: bfloat16 [2, 128, 128], replicated, may hold values from -0.5 to 0.5
- b_mid: float32 [2, 128], replicated, may hold values from -3 to 3
- w_out: bfloat16 [27, 128], replicated, may hold values from -0.5 to 0.5
- b_out: float32 [27], replicated, may hold values from -4 to 4
Outputs:
- relaid: float32 [8192, 27, 128], P(('gx', 'gy'))
The draws below stay inside these ranges and needn't reach their ends.
Inputs may be any that keep to these rules, and one draw needn't show every extreme that they name: Among the 8 x 16 columns of one device, no owner appears more than 8 times, and one owner, the same for every device, appears exactly 8 times on every device.
All inputs are finite; a program needn't handle non-finite values.
Results may differ from the reference program's by a relative error of at most 0.004.
Values sent between devices are 32-bit elements; how exact they have to be, the bound alone decides.
A program may use at most 128 MiB of HBM per device.

```python
import math
import jax
import jax.numpy as jnp
from jax import lax

CX = 8
CY = 16
CZ = 128
HID = 128
MID = 2
STENCIL = 27
NCX = 64
NCY = 64
MOST = 8
N_GX = 8
N_GY = 4


def draw_owner(key, part):
    devices = N_GX * N_GY
    columns = CX * CY
    busiest = jax.random.randint(jax.random.fold_in(key, 7), (), 0, devices)

    def one_device(dev_key):
        first_key, second_key, third_key = jax.random.split(dev_key, 3)
        others = (busiest + 1 + jax.random.permutation(first_key, devices - 1)) % devices
        others_pool = jnp.repeat(others, MOST)
        others_pool = jax.random.permutation(second_key, others_pool)[:columns - MOST]
        listed = jnp.concatenate([jnp.full((MOST,), busiest, jnp.int32), others_pool.astype(jnp.int32)])
        return jax.random.permutation(third_key, listed)
    device_keys = jax.random.split(jax.random.fold_in(key, 11), devices)
    owner_table = jax.vmap(one_device)(device_keys)
    owner_table = owner_table.reshape(N_GX, N_GY, CX, CY).transpose(0, 2, 1, 3).reshape(CX * N_GX, CY * N_GY)
    return owner_table.astype(jnp.int32)


def block_levels(stream_key, shape, cuts, smallest, largest):
    gain, own = 1.0, jax.random.fold_in(stream_key, 6)
    for axis_at, parts in cuts:
        steps = jnp.exp(jax.random.uniform(jax.random.fold_in(own, axis_at), (parts,), jnp.float32, smallest / len(cuts), largest / len(cuts)))
        gain = gain * jnp.repeat(steps, shape[axis_at] // parts).reshape([-1 if axis == axis_at else 1 for axis in range(len(shape))])
    return gain


def normal_values(stream_key, dims, width, limit, kind=jnp.bfloat16):
    drawn = jax.random.normal(stream_key, dims, jnp.float32) * width
    return jnp.minimum(jnp.maximum(drawn, -limit), limit).astype(kind)


def setup_inputs(seed: int = 0) -> dict:
    splits = jax.random.split(jax.random.key(seed), 9)
    return {
        "coefficient": jnp.clip(jnp.exp(math.log(5.0) - 4.6051702 * jax.random.uniform(splits[0], (2, 2, 2, NCX, NCY, CZ), jnp.float32) ** block_levels(splits[0], (2, 2, 2, NCX, NCY, CZ), ((3, 8), (4, 4)), -0.2, 0.2)), 0.05, 5.0),
        "owner": draw_owner(jax.random.fold_in(splits[8], 71), 0),
        "w_in": jnp.clip(jax.random.uniform(splits[2], (HID, STENCIL), jnp.float32, -1.25, 1.25), -1.25, 1.25).astype(jnp.bfloat16),
        "b_in": normal_values(splits[3], (HID,), 0.5, 3.0, jnp.float32),
        "w_mid": normal_values(splits[4], (MID, HID, HID), HID ** -0.5, 0.5),
        "b_mid": normal_values(splits[5], (MID, HID), 0.5, 3.0, jnp.float32),
        "w_out": jnp.clip(jax.random.uniform(splits[6], (STENCIL, HID), jnp.float32, -0.5, 0.5), -0.5, 0.5).astype(jnp.bfloat16),
        "b_out": normal_values(splits[7], (STENCIL,), 1.0, 4.0, jnp.float32),
    }


def offset_list():
    return [(shift_x, shift_y, shift_z) for shift_x in (-1, 0, 1) for shift_y in (-1, 0, 1) for shift_z in (-1, 0, 1)]

def parity_key(offset):
    return tuple((0 if component == 0 else 1 for component in offset))

def shift_next(values, which_axis):
    length = values.shape[which_axis]
    upper_part = lax.slice_in_dim(values, 1, length, axis=which_axis)
    filler = jnp.zeros_like(lax.slice_in_dim(values, 0, 1, axis=which_axis))
    return jnp.concatenate([upper_part, filler], axis=which_axis)

def shift_prev(values, which_axis):
    length = values.shape[which_axis]
    lower_part = lax.slice_in_dim(values, 0, length - 1, axis=which_axis)
    filler = jnp.zeros_like(lax.slice_in_dim(values, 0, 1, axis=which_axis))
    return jnp.concatenate([filler, lower_part], axis=which_axis)

def gather_offsets(fine_field):
    fields = []
    for offset in offset_list():
        portion = fine_field[parity_key(offset)]
        for which_axis, component in enumerate(offset):
            if component == -1:
                portion = shift_prev(portion, which_axis)
        fields.append(portion)
    return fields

def restrict(fine_field, weights):
    fields = gather_offsets(fine_field)
    accumulated = weights[0] * fields[0]
    for index_o in range(1, len(fields)):
        accumulated = accumulated + weights[index_o] * fields[index_o]
    return accumulated

def prolong(weights):
    parity_sums = {}
    for index_o, offset in enumerate(offset_list()):
        portion = weights[index_o]
        for which_axis, component in enumerate(offset):
            if component == -1:
                portion = shift_next(portion, which_axis)
        target = parity_key(offset)
        if target in parity_sums:
            parity_sums[target] = parity_sums[target] + portion
        else:
            parity_sums[target] = portion
    return jnp.stack([jnp.stack([jnp.stack([parity_sums[parity_x, parity_y, parity_z] for parity_z in (0, 1)]) for parity_y in (0, 1)]) for parity_x in (0, 1)])

def step_plus(values, which_axis):
    even_part = lax.slice_in_dim(values, 0, 1, axis=which_axis)
    odd_part = lax.slice_in_dim(values, 1, 2, axis=which_axis)
    return jnp.concatenate([odd_part, shift_next(even_part, which_axis + 3)], axis=which_axis)

def step_minus(values, which_axis):
    even_part = lax.slice_in_dim(values, 0, 1, axis=which_axis)
    odd_part = lax.slice_in_dim(values, 1, 2, axis=which_axis)
    return jnp.concatenate([shift_prev(odd_part, which_axis + 3), even_part], axis=which_axis)

def operate(field, face_coef):
    accumulated = jnp.zeros_like(field)
    for which_axis in range(3):
        face = face_coef[which_axis]
        accumulated = accumulated + face * (field - step_plus(field, which_axis))
        accumulated = accumulated + step_minus(face, which_axis) * (field - step_minus(field, which_axis))
    return accumulated

def pick_offsets(probe_stack):
    for which_axis in range(3):
        grid_shape = [1] * probe_stack.ndim
        grid_shape[which_axis + 3] = probe_stack.shape[which_axis + 3]
        position = lax.broadcasted_iota(jnp.int32, tuple(grid_shape), which_axis + 3)
        picked_rows = []
        for offset in (-1, 0, 1):
            wanted = (position + offset + 3) % 3
            chosen = jnp.zeros_like(lax.slice_in_dim(probe_stack, 0, 1, axis=which_axis))
            for probe_class in range(3):
                chosen = chosen + jnp.where(wanted == probe_class, lax.slice_in_dim(probe_stack, probe_class, probe_class + 1, axis=which_axis), 0.0)
            picked_rows.append(chosen)
        probe_stack = jnp.concatenate(picked_rows, axis=which_axis)
    return probe_stack

def galerkin(weights_ext, kappa_ext):
    face_coef = [jnp.sqrt(kappa_ext * step_plus(kappa_ext, which_axis)) for which_axis in range(3)]
    grid_shape = weights_ext.shape[1:]
    place_x = lax.broadcasted_iota(jnp.int32, grid_shape, 0) % 3
    place_y = lax.broadcasted_iota(jnp.int32, grid_shape, 1) % 3
    place_z = lax.broadcasted_iota(jnp.int32, grid_shape, 2) % 3

    def probe(probe_class, probe_stack):
        chosen = (place_x == probe_class // 9) & (place_y == probe_class // 3 % 3) & (place_z == probe_class % 3)
        masked = jnp.where(chosen[None], weights_ext, 0.0)
        applied = operate(prolong(masked), face_coef)
        return lax.dynamic_update_index_in_dim(probe_stack, restrict(applied, weights_ext), probe_class, 0)
    probe_stack = lax.fori_loop(0, 27, probe, jnp.zeros(weights_ext.shape, jnp.float32))
    picked = pick_offsets(probe_stack.reshape((3, 3, 3) + grid_shape)).reshape(weights_ext.shape)
    return picked[:, 1:-1, 1:-1, 1:-1]

def predict(feature_rows, w_in, b_in, w_mid, b_mid, w_out, b_out):
    hidden = jax.nn.silu(jnp.dot(w_in, feature_rows, preferred_element_type=jnp.float32) + b_in[:, None]).astype(jnp.bfloat16)
    for layer_num in range(w_mid.shape[0]):
        hidden = jax.nn.silu(jnp.dot(w_mid[layer_num], hidden, preferred_element_type=jnp.float32) + b_mid[layer_num][:, None]).astype(jnp.bfloat16)
    return 0.5 * jax.nn.sigmoid(jnp.dot(w_out, hidden, preferred_element_type=jnp.float32) + b_out[:, None])

def reference(coefficient, owner, w_in, b_in, w_mid, b_mid, w_out, b_out):
    kappa_ext = jnp.pad(coefficient, ((0, 0), (0, 0), (0, 0), (1, 1), (1, 1), (1, 1)))
    raw_features = jnp.stack(gather_offsets(jnp.log1p(kappa_ext)))[:, 1:-1, 1:-1, 1:-1]
    feature_grid = raw_features.astype(jnp.bfloat16)

    def per_slab(slab_cells):
        flat_cells = slab_cells.reshape(slab_cells.shape[0], -1)
        return predict(flat_cells, w_in, b_in, w_mid, b_mid, w_out, b_out).reshape(slab_cells.shape)
    weights = jnp.moveaxis(lax.map(per_slab, jnp.moveaxis(feature_grid, 1, 0)), 0, 1)
    weights_ext = jnp.pad(weights, ((0, 0), (1, 1), (1, 1), (1, 1)))
    stencil = galerkin(weights_ext, kappa_ext)
    devices = N_GX * N_GY
    columns = CX * CY
    blocks = stencil.reshape(STENCIL, N_GX, CX, N_GY, CY, CZ).transpose(1, 3, 2, 4, 0, 5).reshape(devices * columns, STENCIL, CZ)
    owners = owner.reshape(N_GX, CX, N_GY, CY).transpose(0, 2, 1, 3).reshape(devices, columns)
    matches = (owners[:, :, None] == jnp.arange(devices, dtype=jnp.int32)[None, None, :]).astype(jnp.int32)
    order_rank = lax.optimization_barrier(jnp.sum(jnp.cumsum(matches, axis=1) * matches, axis=2)) - 1
    source = jnp.arange(devices, dtype=jnp.int32)[:, None]
    slot_index = (owners * (devices * MOST) + source * MOST + order_rank).reshape(-1).astype(jnp.int32)
    relaid = jnp.zeros((devices * devices * MOST, STENCIL, CZ), jnp.float32).at[slot_index].set(blocks)
    return relaid
```

```python
import functools

import jax
import jax.numpy as jnp
import numpy as np
from jax import lax
from jax.experimental import pallas as pl
from jax.experimental.pallas import tpu as pltpu
from jax.sharding import PartitionSpec as P

CORNERS = [(a, b, c) for a in (0, 1) for b in (0, 1) for c in (0, 1)]
OFFSETS = [(a, b, c) for a in (-1, 0, 1) for b in (-1, 0, 1) for c in (-1, 0, 1)]
PAIRS = [(s, t) for s in range(8) for t in range(s, 8)]
PAIR_ROW = {pair: row for row, pair in enumerate(PAIRS)}
POINT_ROWS = 68
FACE_ROWS = 20


def corner_row(corner):
    return corner[0] * 4 + corner[1] * 2 + corner[2]


def point_row(offset):
    return (offset[0] + 1) * 9 + (offset[1] + 1) * 3 + offset[2] + 1


def pair_row(first, second):
    low, high = sorted((corner_row(first), corner_row(second)))
    return PAIR_ROW[low, high]


def edge_form(weight, root, store):
    def value(node, delta):
        offset = tuple(n - 2 * d for n, d in zip(node, delta))
        if min(offset) < -1 or max(offset) > 1:
            return None
        return weight(offset, delta)

    total = {}
    for direction in range(3):
        for node in CORNERS:
            other = tuple(n + (axis == direction) for axis, n in enumerate(node))
            face = root(node) * root(other)
            drops = []
            for delta in CORNERS:
                here, there = value(node, delta), value(other, delta)
                if here is None and there is None:
                    continue
                if there is None:
                    drops.append((delta, here))
                elif here is None:
                    drops.append((delta, -there))
                else:
                    drops.append((delta, here - there))
            for index, (first, drop) in enumerate(drops):
                scaled = face * drop
                for second, other_drop in drops[index:]:
                    row = pair_row(first, second)
                    term = scaled * other_drop
                    total[row] = total[row] + term if row in total else term
    for row, entry in total.items():
        store(row, entry)


SPLITS = (5, 11, 19)


def stencil_kernel(n_gx, n_gy, *refs):
    far, rest = refs[:9], refs[9:]
    out, rest = rest[0], rest[1:]
    low_x, high_x, low_y, high_y, edges, kbuf, logs, roots, wbuf, pairs, blocks, held = rest[:12]
    w_first, w_half, biases, onehot = rest[12:16]
    near = rest[16:25]
    own, owner, pick, w_in, w_mid, w_out, b_in, b_mid, b_out = near
    row_sems, halo_send, halo_recv, send_sems, recv_sems, own_sems = rest[25:]

    _, cx, cy, cz = own.shape
    nx, ny = cx + 4, cy + 4
    wide = cy + 2
    columns = cx * cy
    layers = w_mid.shape[0]
    devices = n_gx * n_gy
    by_point = out.shape[0] == 27
    slots = out.shape[1 if by_point else 0]
    most = slots // devices
    ix, iy = lax.axis_index("gx"), lax.axis_index("gy")
    me = ix * n_gy + iy
    mesh_id = pl.DeviceIdType.MESH
    half = n_gy // 2

    def partner(k):
        across = k // (devices // 2)
        side = (iy // half + 1 + across) % 2
        step = k % (devices // 2)
        return (ix + step % n_gx) % n_gx, side * half + (iy + step // n_gx) % half

    def each(action):
        pl.loop(0, devices // 2)(action)
        pl.loop(devices // 2 + 1, devices)(action)

    barrier = pltpu.get_barrier_semaphore()

    @each
    def _(k):
        px, py = partner(k)
        pl.semaphore_signal(barrier, inc=1, device_id=(px, py), device_id_type=mesh_id)

    fetches = [
        pltpu.make_async_copy(source, target, row_sems.at[number])
        for number, (source, target) in enumerate(zip(far, near))
    ]
    for fetch in fetches:
        fetch.start()

    ways = [(a, b) for a in (-1, 0, 1) for b in (-1, 0, 1) if a or b]

    def exists(way):
        x, y = ix + way[0], iy + way[1]
        return (x >= 0) & (x < n_gx) & (y >= 0) & (y < n_gy)

    def landing(way):
        if way[1] == 0:
            return low_x if way[0] < 0 else high_x
        rim = low_y if way[1] < 0 else high_y
        start = (0, 2, cx + 2)[way[0] + 1]
        return rim.at[:, pl.ds(start, cx if way[0] == 0 else 2)]

    def leaving(way):
        if way[1] == 0:
            return own.at[:, pl.ds(0 if way[0] < 0 else cx - 2, 2)]
        rim = edges.at[0 if way[1] < 0 else 1]
        return rim.at[:, pl.ds(cx - 2 if way[0] > 0 else 0, cx if way[0] == 0 else 2)]

    def halo(number, way):
        return pltpu.make_async_remote_copy(
            src_ref=leaving(way),
            dst_ref=landing((-way[0], -way[1])),
            send_sem=halo_send.at[number],
            recv_sem=halo_recv.at[number],
            device_id=(ix + way[0], iy + way[1]),
            device_id_type=mesh_id,
        )

    for way in ways:
        @pl.when(jnp.logical_not(exists(way)))
        def _(way=way):
            part = landing(way)
            part[...] = jnp.zeros(part.shape, jnp.float32)

    fetches[0].wait()
    edges[0] = own[:, :, :2, :]
    edges[1] = own[:, :, cy - 2:, :]

    lane = lax.broadcasted_iota(jnp.int32, (8, cz), 1)

    def log_rows(x, y):
        kappa = kbuf[pl.ds(pl.multiple_of((x * ny + y) * 8, 8), 8), :]
        value = jnp.log1p(kappa)
        below = jnp.where(lane == 0, 0.0, pltpu.roll(value, 1, 1))
        logs[x * ny + y] = jnp.concatenate([value, below], axis=0).astype(jnp.bfloat16)

    for p in range(8):
        for x in range(2, cx + 2):
            kbuf[pl.ds((x * ny + 2) * 8 + p, cy, stride=8), :] = own[p, x - 2]

    @pl.loop(2, cx + 2)
    def _(x):
        for y in range(2, cy + 2):
            log_rows(x, y)

    pl.semaphore_wait(barrier, devices - 1)
    for number, way in enumerate(ways):
        @pl.when(exists(way))
        def _(number=number, way=way):
            halo(number, way).start()

    for fetch in fetches[1:]:
        fetch.wait()
    w_first[...] = (0.5 * lax.dot_general(
        w_in[...], pick[...], (((0,), (0,)), ((), ())), preferred_element_type=jnp.float32
    )).astype(jnp.bfloat16)
    for m in range(layers):
        w_half[m] = w_mid[m] * jnp.bfloat16(0.5)
    w_half[layers] = jnp.zeros(w_half.shape[1:], jnp.bfloat16)
    w_half[layers, :27] = w_out[...] * jnp.bfloat16(0.5)
    for m in range(layers + 2):
        if m > layers:
            bias = b_out[...]
            rows = 32
            bias = jnp.concatenate([bias, jnp.zeros((1, cz - 27), jnp.float32)], axis=1)
        else:
            bias = b_in[...] if m == 0 else b_mid[m - 1:m, :]
        biases[m] = jnp.transpose(jnp.broadcast_to(0.5 * bias, biases.shape[1:]))

    spread = lax.broadcasted_iota(jnp.int32, (cy, columns), 1) % cy == lax.broadcasted_iota(
        jnp.int32, (cy, columns), 0
    )
    tiled = jnp.dot(
        owner[...].astype(jnp.float32).astype(jnp.bfloat16),
        jnp.where(spread, 1.0, 0.0).astype(jnp.bfloat16),
        preferred_element_type=jnp.float32,
    )
    mine_row = lax.broadcasted_iota(jnp.int32, (cx, columns), 1) // cy == lax.broadcasted_iota(
        jnp.int32, (cx, columns), 0
    )
    owners = jnp.sum(jnp.where(mine_row, tiled, 0.0), axis=0, keepdims=True)
    across = jnp.broadcast_to(owners, (columns, columns))
    earlier = lax.broadcasted_iota(jnp.int32, (columns, columns), 0) < lax.broadcasted_iota(
        jnp.int32, (columns, columns), 1
    )
    same = (across == jnp.transpose(across)) & earlier
    rank = jnp.sum(jnp.where(same, 1.0, 0.0), axis=0, keepdims=True)
    slot = owners * most + rank
    number = lax.broadcasted_iota(jnp.int32, (slots, columns), 0).astype(jnp.float32)
    hit = jnp.where(number == slot, 1.0, 0.0).astype(jnp.bfloat16)
    for third in range(3):
        onehot[:, third * columns:(third + 1) * columns] = hit

    total = (cx + 2) * wide
    group = max(g for g in range(1, 7) if total % g == 0)
    inner = (cx - 1) * (cy - 1)
    lane_out = lax.broadcasted_iota(jnp.int32, (32, cz), 1)

    def place(i):
        j = i - inner
        q = j - 3 * wide
        s, t = j // wide, q % 3
        x = jnp.where(
            q >= 0, 3 + q // 3,
            jnp.where(j >= 0, 1 + s + (cx - 1) * (s // 2), 3 + i // (cy - 1)),
        )
        y = jnp.where(
            q >= 0, 1 + t + (cy - 1) * (t // 2),
            jnp.where(j >= 0, 1 + j % wide, 3 + i % (cy - 1)),
        )
        return x, y

    def activate(value):
        return (value + value * jnp.tanh(value)).astype(jnp.bfloat16)

    def biased(value, m):
        bias = biases[m, :value.shape[0], :]
        return value + jnp.concatenate([bias] * group, axis=1)

    def predict(step):
        places = [place(step * group + k) for k in range(group)]
        parts = []
        for x, y in places:
            at = x * ny + y
            parts.append(
                jnp.concatenate([logs[at], logs[at - ny], logs[at - 1], logs[at - ny - 1]], axis=0)
            )
        rows = jnp.concatenate(parts, axis=1)
        hidden = activate(biased(jnp.dot(w_first[...], rows, preferred_element_type=jnp.float32), 0))
        for m in range(layers):
            hidden = activate(
                biased(jnp.dot(w_half[m], hidden, preferred_element_type=jnp.float32), m + 1)
            )
        last = jnp.dot(w_half[layers, :32], hidden, preferred_element_type=jnp.float32)
        weights = 0.25 + 0.25 * jnp.tanh(biased(last, layers + 1))
        for k, (x, y) in enumerate(places):
            outside = (
                ((x == 1) & (ix == 0))
                | ((x == cx + 2) & (ix == n_gx - 1))
                | ((y == 1) & (iy == 0))
                | ((y == cy + 2) & (iy == n_gy - 1))
            )
            keep = jnp.where(outside, 0.0, 1.0)
            column = weights[:, k * cz:(k + 1) * cz] * keep
            above = jnp.where(lane_out == cz - 1, 0.0, pltpu.roll(column, cz - 1, 1))
            row = ((x - 1) * wide + y - 1) * POINT_ROWS
            wbuf[pl.ds(row, 32), :] = column
            wbuf[pl.ds(row + 32, 32), :] = above

    pl.loop(0, inner // group)(predict)

    for number, way in enumerate(ways):
        @pl.when(exists(way))
        def _(number=number, way=way):
            halo(number, way).wait_send()

        @pl.when(exists((-way[0], -way[1])))
        def _(number=number, way=way):
            halo(number, way).wait_recv()

    for p in range(8):
        for x in range(nx):
            start = x * ny * 8 + p
            if x < 2 or x >= cx + 2:
                middle = low_x[p, x] if x < 2 else high_x[p, x - 2 - cx]
                kbuf[pl.ds(start + 16, cy, stride=8), :] = middle
            kbuf[pl.ds(start, 2, stride=8), :] = low_y[p, x]
            kbuf[pl.ds(start + (cy + 2) * 8, 2, stride=8), :] = high_y[p, x]

    @pl.loop(0, 4)
    def _(s):
        x = s + cx * (s // 2)
        for y in range(ny):
            log_rows(x, y)

    @pl.loop(2, cx + 2)
    def _(x):
        for y in (0, 1, cy + 2, cy + 3):
            log_rows(x, y)

    @pl.loop(1, nx - 1)
    def _(x):
        for y in range(1, ny - 1):
            root = jnp.sqrt(kbuf[pl.ds(pl.multiple_of((x * ny + y) * 8, 8), 8), :])
            above = jnp.where(lane == cz - 1, 0.0, pltpu.roll(root, cz - 1, 1))
            row = ((x - 1) * wide + y - 1) * FACE_ROWS
            roots[pl.ds(row, 8), :] = root
            roots[pl.ds(row + 8, 8), :] = above

    pl.loop(inner // group, total // group)(predict)

    @pl.loop(0, pl.cdiv((cx + 1) * wide, 8))
    def _(tile):
        base = tile * 8

        def weight(offset, delta):
            column = base + delta[0] * wide + delta[1]
            row = point_row(offset) + 32 * delta[2]
            return wbuf[pl.ds(column * POINT_ROWS + row, 8, stride=POINT_ROWS), :]

        def root(node):
            column = base + node[0] // 2 * wide + node[1] // 2
            row = corner_row(tuple(n % 2 for n in node)) + 8 * (node[2] // 2)
            return roots[pl.ds(column * FACE_ROWS + row, 8, stride=FACE_ROWS), :]

        def store(row, entry):
            pairs[pl.ds(base * len(PAIRS) + row, 8, stride=len(PAIRS)), :] = entry

        edge_form(weight, root, store)

    def lay(first_row, last_row):
        @pl.loop(0, cx * (cy // 8))
        def _(tile):
            x = tile // (cy // 8)
            y = tile % (cy // 8) * 8
            cell = (x + 1) * wide + y + 1
            for number in range(first_row, last_row):
                offset = OFFSETS[number]
                sums = [None, None]
                for first in CORNERS:
                    second = tuple(f + o for f, o in zip(first, offset))
                    if min(second) < 0 or max(second) > 1:
                        continue
                    base = cell - first[0] * wide - first[1]
                    start = base * len(PAIRS) + pair_row(first, second)
                    entry = pairs[pl.ds(start, 8, stride=len(PAIRS)), :]
                    seen = sums[first[2]]
                    sums[first[2]] = entry if seen is None else seen + entry
                if sums[1] is not None:
                    moved = pltpu.roll(sums[1], 1, 1)
                    sums[0] = moved if sums[0] is None else sums[0] + moved
                blocks[number, pl.ds(pl.multiple_of(x * cy + y, 8), 8), :] = sums[0]

        @pl.loop(first_row, last_row)
        def _(number):
            block = blocks[number]
            top = block.astype(jnp.bfloat16)
            left = block - top.astype(jnp.float32)
            middle = left.astype(jnp.bfloat16)
            bottom = (left - middle.astype(jnp.float32)).astype(jnp.bfloat16)
            placed = jnp.dot(
                onehot[...],
                jnp.concatenate([top, middle, bottom], axis=0),
                preferred_element_type=jnp.float32,
            )
            if by_point:
                held[number] = placed
            else:
                held[:, number, :] = placed

    bounds = (0, *SPLITS, 27) if by_point else (0, 27)

    def slots_of(ref, part, device):
        if by_point:
            rows = pl.ds(bounds[part], bounds[part + 1] - bounds[part])
            return ref.at[rows, pl.ds(pl.multiple_of(device * most, 8), most)]
        return ref.at[pl.ds(device * most, most)]

    def copy(part, k, home):
        px, py = partner(k)
        other = px * n_gy + py
        return pltpu.make_async_remote_copy(
            src_ref=slots_of(held, part, other),
            dst_ref=slots_of(out, part, home),
            send_sem=send_sems.at[part, other],
            recv_sem=recv_sems.at[part, home],
            device_id=(px, py),
            device_id_type=mesh_id,
        )

    def stay(part):
        return pltpu.make_async_copy(
            slots_of(held, part, me), slots_of(out, part, me), own_sems.at[part]
        )

    for part in range(len(bounds) - 1):
        lay(bounds[part], bounds[part + 1])

        @each
        def _(k, part=part):
            copy(part, k, me).start()

        stay(part).start()

    for part in range(len(bounds) - 1):
        @each
        def _(k, part=part):
            px, py = partner(k)
            copy(part, k, me).wait_send()
            copy(part, k, px * n_gy + py).wait_recv()

        stay(part).wait()


def per_device(coefficient, owner, w_in, b_in, w_mid, b_mid, w_out, b_out):
    cx, cy, cz = coefficient.shape[3:]
    hid = w_in.shape[0]
    n_gx, n_gy = lax.axis_size("gx"), lax.axis_size("gy")
    devices = n_gx * n_gy
    columns = cx * cy
    most = 2 * columns // devices
    slots = devices * most

    pick = np.zeros((27, 64), np.float32)
    row = 0
    for dx, dy in ((0, 0), (1, 0), (0, 1), (1, 1)):
        for dz in (0, 1):
            for corner in CORNERS:
                shift = (dx, dy, dz)
                if all(s <= c for s, c in zip(shift, corner)):
                    pick[point_row(tuple(c - 2 * s for s, c in zip(shift, corner))), row] = 1.0
                row += 1

    wide = cy + 2
    tiles = -(-((cx + 1) * wide) // 8) * 8
    spread = max((cx + 2) * wide, tiles + wide + 2)
    small = (
        coefficient.reshape(8, cx, cy, cz), owner, jnp.asarray(pick, jnp.bfloat16),
        w_in.T, w_mid, w_out, b_in[None, :], b_mid, b_out[None, :],
    )
    by_point = most % 8 == 0
    shape = (27, slots, cz) if by_point else (slots, 27, cz)
    parts = len(SPLITS) + 1 if by_point else 1
    f32, bf16 = jnp.float32, jnp.bfloat16
    relaid = pl.pallas_call(
        functools.partial(stencil_kernel, n_gx, n_gy),
        out_shape=jax.ShapeDtypeStruct(shape, f32),
        in_specs=[pl.BlockSpec(memory_space=pltpu.HBM)] * len(small),
        out_specs=pl.BlockSpec(memory_space=pl.ANY),
        scratch_shapes=[
            pltpu.VMEM((8, 2, cy, cz), f32),
            pltpu.VMEM((8, 2, cy, cz), f32),
            pltpu.VMEM((8, cx + 4, 2, cz), f32),
            pltpu.VMEM((8, cx + 4, 2, cz), f32),
            pltpu.VMEM((2, 8, cx, 2, cz), f32),
            pltpu.VMEM(((cx + 4) * (cy + 4) * 8 + 8, cz), f32),
            pltpu.VMEM(((cx + 4) * (cy + 4), 16, cz), bf16),
            pltpu.VMEM(((spread + 1) * FACE_ROWS, cz), f32),
            pltpu.VMEM(((spread + 1) * POINT_ROWS, cz), f32),
            pltpu.VMEM(((tiles + 1) * len(PAIRS), cz), f32),
            pltpu.VMEM((27, columns, cz), f32),
            pltpu.VMEM(shape, f32),
            pltpu.VMEM((hid, 64), bf16),
            pltpu.VMEM((w_mid.shape[0] + 1, hid, hid), bf16),
            pltpu.VMEM((w_mid.shape[0] + 2, hid, cz), f32),
            pltpu.VMEM((slots, 3 * columns), bf16),
            *[pltpu.VMEM(part.shape, part.dtype) for part in small],
            pltpu.SemaphoreType.DMA((len(small),)),
            pltpu.SemaphoreType.DMA((8,)),
            pltpu.SemaphoreType.DMA((8,)),
            pltpu.SemaphoreType.DMA((parts, devices)),
            pltpu.SemaphoreType.DMA((parts, devices)),
            pltpu.SemaphoreType.DMA((parts,)),
        ],
        compiler_params=pltpu.CompilerParams(
            collective_id=0, has_side_effects=True, vmem_limit_bytes=60 << 20
        ),
        name="stencil",
    )(*small)
    return jnp.transpose(relaid, (1, 0, 2)) if by_point else relaid


def solution(mesh):
    return jax.shard_map(
        per_device,
        mesh=mesh,
        in_specs=(
            P(None, None, None, "gx", "gy", None),
            P("gx", "gy"),
            P(),
            P(),
            P(),
            P(),
            P(),
            P(),
        ),
        out_specs=P(("gx", "gy"), None, None),
        check_vma=False,
    )
```

```python
import functools

import jax
import jax.numpy as jnp
import numpy as np
from jax import lax
from jax.experimental import pallas as pl
from jax.experimental.pallas import tpu as pltpu
from jax.sharding import PartitionSpec as P

CORNERS = [(a, b, c) for a in (0, 1) for b in (0, 1) for c in (0, 1)]
OFFSETS = [(a, b, c) for a in (-1, 0, 1) for b in (-1, 0, 1) for c in (-1, 0, 1)]
PAIRS = [(s, t) for s in range(8) for t in range(s, 8)]
PAIR_ROW = {pair: row for row, pair in enumerate(PAIRS)}
POINT_ROWS = 68
FACE_ROWS = 20


def corner_row(corner):
    return corner[0] * 4 + corner[1] * 2 + corner[2]


def point_row(offset):
    return (offset[0] + 1) * 9 + (offset[1] + 1) * 3 + offset[2] + 1


def pair_row(first, second):
    low, high = sorted((corner_row(first), corner_row(second)))
    return PAIR_ROW[low, high]


def edge_form(weight, root, store):
    def value(node, delta):
        offset = tuple(n - 2 * d for n, d in zip(node, delta))
        if min(offset) < -1 or max(offset) > 1:
            return None
        return weight(offset, delta)

    total = {}
    for direction in range(3):
        for node in CORNERS:
            other = tuple(n + (axis == direction) for axis, n in enumerate(node))
            face = root(node) * root(other)
            drops = []
            for delta in CORNERS:
                here, there = value(node, delta), value(other, delta)
                if here is None and there is None:
                    continue
                if there is None:
                    drops.append((delta, here))
                elif here is None:
                    drops.append((delta, -there))
                else:
                    drops.append((delta, here - there))
            for index, (first, drop) in enumerate(drops):
                scaled = face * drop
                for second, other_drop in drops[index:]:
                    row = pair_row(first, second)
                    term = scaled * other_drop
                    total[row] = total[row] + term if row in total else term
    for row, entry in total.items():
        store(row, entry)


SPLITS = (5, 11, 19)


def stencil_kernel(n_gx, n_gy, *refs):
    far, rest = refs[:9], refs[9:]
    out, rest = rest[0], rest[1:]
    low_x, high_x, low_y, high_y, edges, kbuf, logs, roots, wbuf, pairs, blocks, held = rest[:12]
    w_first, w_half, biases, onehot = rest[12:16]
    near = rest[16:25]
    stages = rest[25:25 + near[4].shape[0] + 1]
    rest = rest[25 + len(stages):]
    own, owner, pick, w_in, w_mid, w_out, b_in, b_mid, b_out = near
    row_sems, halo_send, halo_recv, send_sems, recv_sems, own_sems = rest

    _, cx, cy, cz = own.shape
    nx, ny = cx + 4, cy + 4
    wide = cy + 2
    columns = cx * cy
    layers = w_mid.shape[0]
    devices = n_gx * n_gy
    by_point = out.shape[0] == 27
    slots = out.shape[1 if by_point else 0]
    most = slots // devices
    ix, iy = lax.axis_index("gx"), lax.axis_index("gy")
    me = ix * n_gy + iy
    mesh_id = pl.DeviceIdType.MESH
    half = n_gy // 2

    def partner(k):
        across = k // (devices // 2)
        side = (iy // half + 1 + across) % 2
        step = k % (devices // 2)
        return (ix + step % n_gx) % n_gx, side * half + (iy + step // n_gx) % half

    def each(action):
        pl.loop(0, devices // 2)(action)
        pl.loop(devices // 2 + 1, devices)(action)

    barrier = pltpu.get_barrier_semaphore()

    @each
    def _(k):
        px, py = partner(k)
        pl.semaphore_signal(barrier, inc=1, device_id=(px, py), device_id_type=mesh_id)

    fetches = [
        pltpu.make_async_copy(source, target, row_sems.at[number])
        for number, (source, target) in enumerate(zip(far, near))
    ]
    for fetch in fetches:
        fetch.start()

    ways = [(a, b) for a in (-1, 0, 1) for b in (-1, 0, 1) if a or b]

    def exists(way):
        x, y = ix + way[0], iy + way[1]
        return (x >= 0) & (x < n_gx) & (y >= 0) & (y < n_gy)

    def landing(way):
        if way[1] == 0:
            return low_x if way[0] < 0 else high_x
        rim = low_y if way[1] < 0 else high_y
        start = (0, 2, cx + 2)[way[0] + 1]
        return rim.at[:, pl.ds(start, cx if way[0] == 0 else 2)]

    def leaving(way):
        if way[1] == 0:
            return own.at[:, pl.ds(0 if way[0] < 0 else cx - 2, 2)]
        rim = edges.at[0 if way[1] < 0 else 1]
        return rim.at[:, pl.ds(cx - 2 if way[0] > 0 else 0, cx if way[0] == 0 else 2)]

    def halo(number, way):
        return pltpu.make_async_remote_copy(
            src_ref=leaving(way),
            dst_ref=landing((-way[0], -way[1])),
            send_sem=halo_send.at[number],
            recv_sem=halo_recv.at[number],
            device_id=(ix + way[0], iy + way[1]),
            device_id_type=mesh_id,
        )

    for way in ways:
        @pl.when(jnp.logical_not(exists(way)))
        def _(way=way):
            part = landing(way)
            part[...] = jnp.zeros(part.shape, jnp.float32)

    fetches[0].wait()
    edges[0] = own[:, :, :2, :]
    edges[1] = own[:, :, cy - 2:, :]

    lane = lax.broadcasted_iota(jnp.int32, (8, cz), 1)

    def log_rows(x, y):
        kappa = kbuf[pl.ds(pl.multiple_of((x * ny + y) * 8, 8), 8), :]
        value = jnp.log1p(kappa)
        below = jnp.where(lane == 0, 0.0, pltpu.roll(value, 1, 1))
        logs[x * ny + y] = jnp.concatenate([value, below], axis=0).astype(jnp.bfloat16)

    for p in range(8):
        for x in range(2, cx + 2):
            kbuf[pl.ds((x * ny + 2) * 8 + p, cy, stride=8), :] = own[p, x - 2]

    @pl.loop(2, cx + 2)
    def _(x):
        for y in range(2, cy + 2):
            log_rows(x, y)

    pl.semaphore_wait(barrier, devices - 1)
    for number, way in enumerate(ways):
        @pl.when(exists(way))
        def _(number=number, way=way):
            halo(number, way).start()

    for fetch in fetches[1:]:
        fetch.wait()
    w_first[...] = (0.5 * lax.dot_general(
        w_in[...], pick[...], (((0,), (0,)), ((), ())), preferred_element_type=jnp.float32
    )).astype(jnp.bfloat16)
    for m in range(layers):
        w_half[m] = w_mid[m] * jnp.bfloat16(0.5)
    w_half[layers] = jnp.zeros(w_half.shape[1:], jnp.bfloat16)
    w_half[layers, :27] = w_out[...] * jnp.bfloat16(0.5)
    for m in range(layers + 2):
        if m > layers:
            bias = b_out[...]
            rows = 32
            bias = jnp.concatenate([bias, jnp.zeros((1, cz - 27), jnp.float32)], axis=1)
        else:
            bias = b_in[...] if m == 0 else b_mid[m - 1:m, :]
        biases[m] = jnp.transpose(jnp.broadcast_to(0.5 * bias, biases.shape[1:]))

    spread = lax.broadcasted_iota(jnp.int32, (cy, columns), 1) % cy == lax.broadcasted_iota(
        jnp.int32, (cy, columns), 0
    )
    tiled = jnp.dot(
        owner[...].astype(jnp.float32).astype(jnp.bfloat16),
        jnp.where(spread, 1.0, 0.0).astype(jnp.bfloat16),
        preferred_element_type=jnp.float32,
    )
    mine_row = lax.broadcasted_iota(jnp.int32, (cx, columns), 1) // cy == lax.broadcasted_iota(
        jnp.int32, (cx, columns), 0
    )
    owners = jnp.sum(jnp.where(mine_row, tiled, 0.0), axis=0, keepdims=True)
    across = jnp.broadcast_to(owners, (columns, columns))
    earlier = lax.broadcasted_iota(jnp.int32, (columns, columns), 0) < lax.broadcasted_iota(
        jnp.int32, (columns, columns), 1
    )
    same = (across == jnp.transpose(across)) & earlier
    rank = jnp.sum(jnp.where(same, 1.0, 0.0), axis=0, keepdims=True)
    slot = owners * most + rank
    number = lax.broadcasted_iota(jnp.int32, (slots, columns), 0).astype(jnp.float32)
    hit = jnp.where(number == slot, 1.0, 0.0).astype(jnp.bfloat16)
    for third in range(3):
        onehot[:, third * columns:(third + 1) * columns] = hit

    total = (cx + 2) * wide
    group = max(g for g in range(1, 7) if total % g == 0)
    inner = (cx - 1) * (cy - 1)
    lane_out = lax.broadcasted_iota(jnp.int32, (32, cz), 1)

    bands = inner // group
    period = 2 * (cy - 1) // group
    turn = (cx - 1) * wide // group
    lines = wide // group
    assert period * group == 2 * (cy - 1) and turn * group == (cx - 1) * wide
    assert lines * group == wide and group % 3 == 0

    def places(step):
        block = step // period
        start = (step - block * period) * group
        rim = step - turn
        line = rim // lines
        rim_x = 1 + line + (cx - 1) * (line // 2)
        rim_y = 1 + (rim - line * lines) * group
        found = []
        for k in range(group):
            at = start + k
            second = (at >= cy - 1).astype(jnp.int32)
            x, y = 3 + 2 * block + second, 3 + at - (cy - 1) * second
            behind = inner % group
            t = (k - behind) % 3
            side = step >= bands + (0 if k >= behind else 1)
            side_x = 3 + (group // 3) * (step - bands) + (k - behind) // 3
            x = jnp.where(side, side_x, x)
            y = jnp.where(side, 1 + t + (cy - 1) * (t // 2), y)
            found.append((jnp.where(rim >= 0, rim_x, x), jnp.where(rim >= 0, rim_y + k, y)))
        return found

    def activate(value):
        return (value + value * jnp.tanh(value)).astype(jnp.bfloat16)

    def biased(value, m):
        bias = biases[m, :value.shape[0], :]
        return value + jnp.concatenate([bias] * group, axis=1)

    steps = total // group

    def predict(tick):
        hidden = stages[layers]
        last = jnp.dot(w_half[layers, :32], hidden[...], preferred_element_type=jnp.float32)
        weights = 0.25 + 0.25 * jnp.tanh(biased(last, layers + 1))
        done = jnp.maximum(tick - layers - 1, 0)
        for k, (x, y) in enumerate(places(done)):
            outside = (
                ((x == 1) & (ix == 0))
                | ((x == cx + 2) & (ix == n_gx - 1))
                | ((y == 1) & (iy == 0))
                | ((y == cy + 2) & (iy == n_gy - 1))
            )
            keep = jnp.where(outside, 0.0, 1.0)
            column = weights[:, k * cz:(k + 1) * cz] * keep
            above = jnp.where(lane_out == cz - 1, 0.0, pltpu.roll(column, cz - 1, 1))
            row = ((x - 1) * wide + y - 1) * POINT_ROWS
            wbuf[pl.ds(row, 32), :] = column
            wbuf[pl.ds(row + 32, 32), :] = above
        for m in reversed(range(layers)):
            stages[m + 1][...] = activate(
                biased(jnp.dot(w_half[m], stages[m][...], preferred_element_type=jnp.float32), m + 1)
            )
        fresh = jnp.minimum(tick, steps - 1)
        parts = []
        for x, y in places(fresh):
            at = x * ny + y
            parts.append(
                jnp.concatenate([logs[at], logs[at - ny], logs[at - 1], logs[at - ny - 1]], axis=0)
            )
        rows = jnp.concatenate(parts, axis=1)
        stages[0][...] = activate(
            biased(jnp.dot(w_first[...], rows, preferred_element_type=jnp.float32), 0)
        )

    for stage in stages:
        stage[...] = jnp.zeros(stage.shape, stage.dtype)

    pl.loop(0, inner // group)(predict)

    for number, way in enumerate(ways):
        @pl.when(exists(way))
        def _(number=number, way=way):
            halo(number, way).wait_send()

        @pl.when(exists((-way[0], -way[1])))
        def _(number=number, way=way):
            halo(number, way).wait_recv()

    for p in range(8):
        for x in range(nx):
            start = x * ny * 8 + p
            if x < 2 or x >= cx + 2:
                middle = low_x[p, x] if x < 2 else high_x[p, x - 2 - cx]
                kbuf[pl.ds(start + 16, cy, stride=8), :] = middle
            kbuf[pl.ds(start, 2, stride=8), :] = low_y[p, x]
            kbuf[pl.ds(start + (cy + 2) * 8, 2, stride=8), :] = high_y[p, x]

    @pl.loop(0, 4)
    def _(s):
        x = s + cx * (s // 2)
        for y in range(ny):
            log_rows(x, y)

    @pl.loop(2, cx + 2)
    def _(x):
        for y in (0, 1, cy + 2, cy + 3):
            log_rows(x, y)

    @pl.loop(1, nx - 1)
    def _(x):
        for y in range(1, ny - 1):
            root = jnp.sqrt(kbuf[pl.ds(pl.multiple_of((x * ny + y) * 8, 8), 8), :])
            above = jnp.where(lane == cz - 1, 0.0, pltpu.roll(root, cz - 1, 1))
            row = ((x - 1) * wide + y - 1) * FACE_ROWS
            roots[pl.ds(row, 8), :] = root
            roots[pl.ds(row + 8, 8), :] = above

    pl.loop(inner // group, steps + layers + 1)(predict)

    @pl.loop(0, pl.cdiv((cx + 1) * wide, 8))
    def _(tile):
        base = tile * 8

        def weight(offset, delta):
            column = base + delta[0] * wide + delta[1]
            row = point_row(offset) + 32 * delta[2]
            return wbuf[pl.ds(column * POINT_ROWS + row, 8, stride=POINT_ROWS), :]

        def root(node):
            column = base + node[0] // 2 * wide + node[1] // 2
            row = corner_row(tuple(n % 2 for n in node)) + 8 * (node[2] // 2)
            return roots[pl.ds(column * FACE_ROWS + row, 8, stride=FACE_ROWS), :]

        def store(row, entry):
            pairs[pl.ds(base * len(PAIRS) + row, 8, stride=len(PAIRS)), :] = entry

        edge_form(weight, root, store)

    def lay(first_row, last_row):
        @pl.loop(0, cx * (cy // 8))
        def _(tile):
            x = tile // (cy // 8)
            y = tile % (cy // 8) * 8
            cell = (x + 1) * wide + y + 1
            for number in range(first_row, last_row):
                offset = OFFSETS[number]
                sums = [None, None]
                for first in CORNERS:
                    second = tuple(f + o for f, o in zip(first, offset))
                    if min(second) < 0 or max(second) > 1:
                        continue
                    base = cell - first[0] * wide - first[1]
                    start = base * len(PAIRS) + pair_row(first, second)
                    entry = pairs[pl.ds(start, 8, stride=len(PAIRS)), :]
                    seen = sums[first[2]]
                    sums[first[2]] = entry if seen is None else seen + entry
                if sums[1] is not None:
                    moved = pltpu.roll(sums[1], 1, 1)
                    sums[0] = moved if sums[0] is None else sums[0] + moved
                blocks[number, pl.ds(pl.multiple_of(x * cy + y, 8), 8), :] = sums[0]

        @pl.loop(first_row, last_row)
        def _(number):
            block = blocks[number]
            top = block.astype(jnp.bfloat16)
            left = block - top.astype(jnp.float32)
            middle = left.astype(jnp.bfloat16)
            bottom = (left - middle.astype(jnp.float32)).astype(jnp.bfloat16)
            placed = jnp.dot(
                onehot[...],
                jnp.concatenate([top, middle, bottom], axis=0),
                preferred_element_type=jnp.float32,
            )
            if by_point:
                held[number] = placed
            else:
                held[:, number, :] = placed

    bounds = (0, *SPLITS, 27) if by_point else (0, 27)

    def slots_of(ref, part, device):
        if by_point:
            rows = pl.ds(bounds[part], bounds[part + 1] - bounds[part])
            return ref.at[rows, pl.ds(pl.multiple_of(device * most, 8), most)]
        return ref.at[pl.ds(device * most, most)]

    def copy(part, k, home):
        px, py = partner(k)
        other = px * n_gy + py
        return pltpu.make_async_remote_copy(
            src_ref=slots_of(held, part, other),
            dst_ref=slots_of(out, part, home),
            send_sem=send_sems.at[part, other],
            recv_sem=recv_sems.at[part, home],
            device_id=(px, py),
            device_id_type=mesh_id,
        )

    def stay(part):
        return pltpu.make_async_copy(
            slots_of(held, part, me), slots_of(out, part, me), own_sems.at[part]
        )

    for part in range(len(bounds) - 1):
        lay(bounds[part], bounds[part + 1])

        @each
        def _(k, part=part):
            copy(part, k, me).start()

        stay(part).start()

    for part in range(len(bounds) - 1):
        @each
        def _(k, part=part):
            px, py = partner(k)
            copy(part, k, me).wait_send()
            copy(part, k, px * n_gy + py).wait_recv()

        stay(part).wait()


def per_device(coefficient, owner, w_in, b_in, w_mid, b_mid, w_out, b_out):
    cx, cy, cz = coefficient.shape[3:]
    hid = w_in.shape[0]
    n_gx, n_gy = lax.axis_size("gx"), lax.axis_size("gy")
    devices = n_gx * n_gy
    columns = cx * cy
    most = 2 * columns // devices
    slots = devices * most

    pick = np.zeros((27, 64), np.float32)
    row = 0
    for dx, dy in ((0, 0), (1, 0), (0, 1), (1, 1)):
        for dz in (0, 1):
            for corner in CORNERS:
                shift = (dx, dy, dz)
                if all(s <= c for s, c in zip(shift, corner)):
                    pick[point_row(tuple(c - 2 * s for s, c in zip(shift, corner))), row] = 1.0
                row += 1

    wide = cy + 2
    tiles = -(-((cx + 1) * wide) // 8) * 8
    spread = max((cx + 2) * wide, tiles + wide + 2)
    small = (
        coefficient.reshape(8, cx, cy, cz), owner, jnp.asarray(pick, jnp.bfloat16),
        w_in.T, w_mid, w_out, b_in[None, :], b_mid, b_out[None, :],
    )
    group = max(g for g in range(1, 7) if (cx + 2) * wide % g == 0)
    by_point = most % 8 == 0
    shape = (27, slots, cz) if by_point else (slots, 27, cz)
    parts = len(SPLITS) + 1 if by_point else 1
    f32, bf16 = jnp.float32, jnp.bfloat16
    relaid = pl.pallas_call(
        functools.partial(stencil_kernel, n_gx, n_gy),
        out_shape=jax.ShapeDtypeStruct(shape, f32),
        in_specs=[pl.BlockSpec(memory_space=pltpu.HBM)] * len(small),
        out_specs=pl.BlockSpec(memory_space=pl.ANY),
        scratch_shapes=[
            pltpu.VMEM((8, 2, cy, cz), f32),
            pltpu.VMEM((8, 2, cy, cz), f32),
            pltpu.VMEM((8, cx + 4, 2, cz), f32),
            pltpu.VMEM((8, cx + 4, 2, cz), f32),
            pltpu.VMEM((2, 8, cx, 2, cz), f32),
            pltpu.VMEM(((cx + 4) * (cy + 4) * 8 + 8, cz), f32),
            pltpu.VMEM(((cx + 4) * (cy + 4), 16, cz), bf16),
            pltpu.VMEM(((spread + 1) * FACE_ROWS, cz), f32),
            pltpu.VMEM(((spread + 1) * POINT_ROWS, cz), f32),
            pltpu.VMEM(((tiles + 1) * len(PAIRS), cz), f32),
            pltpu.VMEM((27, columns, cz), f32),
            pltpu.VMEM(shape, f32),
            pltpu.VMEM((hid, 64), bf16),
            pltpu.VMEM((w_mid.shape[0] + 1, hid, hid), bf16),
            pltpu.VMEM((w_mid.shape[0] + 2, hid, cz), f32),
            pltpu.VMEM((slots, 3 * columns), bf16),
            *[pltpu.VMEM(part.shape, part.dtype) for part in small],
            *[pltpu.VMEM((hid, group * cz), bf16)] * (w_mid.shape[0] + 1),
            pltpu.SemaphoreType.DMA((len(small),)),
            pltpu.SemaphoreType.DMA((8,)),
            pltpu.SemaphoreType.DMA((8,)),
            pltpu.SemaphoreType.DMA((parts, devices)),
            pltpu.SemaphoreType.DMA((parts, devices)),
            pltpu.SemaphoreType.DMA((parts,)),
        ],
        compiler_params=pltpu.CompilerParams(
            collective_id=0, has_side_effects=True, vmem_limit_bytes=28 << 20
        ),
        name="stencil",
    )(*small)
    return jnp.transpose(relaid, (1, 0, 2)) if by_point else relaid


def solution(mesh):
    return jax.shard_map(
        per_device,
        mesh=mesh,
        in_specs=(
            P(None, None, None, "gx", "gy", None),
            P("gx", "gy"),
            P(),
            P(),
            P(),
            P(),
            P(),
            P(),
        ),
        out_specs=P(("gx", "gy"), None, None),
        check_vma=False,
    )
```
